128 devices in a mesh: dp: 4 (over x), expert: 32 (over z, y, core).
Axes of the slice: x: 4, y: 4, z: 4, core: 2. Of those that a mesh axis runs over, the one named last changes fastest.
Arguments:
- tokens: bfloat16 [8192, 2048], P(('dp', 'expert')), may hold values from -6 to 6
- out_grad: bfloat16 [8192, 2048], P(('dp', 'expert')), may hold values from -6 to 6
- expert_ids: int32 [8192, 6], P(('dp', 'expert')), may hold values from 0 to 31, all different within a row; in each aligned block of 64 rows (0 to 63, 64 to 127, ...) at most 20 rows name the same one
- gates: float32 [8192, 6], P(('dp', 'expert')), may hold values from 0.1 to 1
- w_gate: bfloat16 [32, 1408, 2048], P('expert', 'dp'), may hold values from -0.125 to 0.125
- w_up: bfloat16 [32, 1408, 2048], P('expert', 'dp'), may hold values from -0.125 to 0.125
- w_down: bfloat16 [32, 1408, 2048], P('expert', 'dp'), may hold values from -0.15625 to 0.15625
Outputs:
- grad_tokens: bfloat16 [8192, 2048], P(('dp', 'expert'))
- grad_gate: bfloat16 [32, 1408, 2048], P('expert', 'dp')
- grad_up: bfloat16 [32, 1408, 2048], P('expert', 'dp')
- grad_down: bfloat16 [32, 1408, 2048], P('expert', 'dp')
The draws below stay inside these ranges and needn't reach their ends.
Inputs may be any that keep to these rules, and one draw needn't show every extreme that they name: `expert_ids`: each token names 6 different experts. Among the rows of one device, no expert is named by more than 20 tokens, a bound that some block reaches.
All inputs are finite; a program needn't handle non-finite values.
Results may differ from the reference program's by a relative error of at most 0.012.
Values may be sent and summed in bfloat16 or wider, within the bound.
No kernel may reach another device: no remote copies, remote signals or barrier semaphores. Data moves between devices by JAX's collectives and lax.ppermute only.
A program may use at most 128 MiB of HBM per device.

```python
import math
import jax
import jax.numpy as jnp
import numpy as np
from jax import lax

D = 2048
FF = 1408
TOPK = 6
TOK_DEV = 64
EXPERTS = 32
CAP = 20
TOKENS = 8192
N_DP = 4
N_EXPERT = 32


def shard_levels(stream_key, dims, pieces, smallest, top_value):
    gain, own = 1.0, jax.random.fold_in(stream_key, 6)
    for dim, shards_of in pieces:
        steps = jnp.exp(jax.random.uniform(jax.random.fold_in(own, dim), (shards_of,), jnp.float32, smallest / len(pieces), top_value / len(pieces)))
        gain = gain * jnp.repeat(steps, dims[dim] // shards_of).reshape([-1 if axis == dim else 1 for axis in range(len(dims))])
    return gain


def shared_out(key, own, number, rows, count, top, limit, slope):
    order = jax.random.permutation(key, count)
    heavy_load, usual = load_shares(count, rows * top, limit, slope, True), load_shares(count, rows * top, limit, slope, False)
    places = jnp.arange(count)

    def named(sizes, offset_by):
        used = int((sizes > 0).sum())
        fixed = max(1, used // 4)
        moved = fixed + (places - fixed + offset_by * (used - fixed)) % max(1, count - fixed)
        return jnp.zeros((count,), jnp.int32).at[order[jnp.where(places < fixed, places, moved)]].set(jnp.asarray(sizes, jnp.int32))

    sizes = jnp.where(number % 4 == 0, named(heavy_load, number // 4), named(usual, number - number // 4 - 1))
    mixed = jax.random.permutation(jax.random.fold_in(own, 3), count)
    giver, receiver = mixed[0:count // 2 * 2:2], mixed[1:count // 2 * 2:2]
    margin = jnp.minimum(sizes[giver] - 1, limit - sizes[receiver]) // 2
    margin = jnp.where((giver == order[0]) | (receiver == order[0]) | (sizes[receiver] == 0), 0, jnp.maximum(margin, 0))
    moved = jax.random.randint(jax.random.fold_in(own, 4), (count // 2,), 0, 1 << 20) % (margin + 1)
    sizes = sizes.at[giver].add(-moved).at[receiver].add(moved)
    members = jnp.searchsorted(jnp.cumsum(sizes), jnp.arange(rows * top), side="right").astype(jnp.int32)
    listing = members.reshape(top, rows).T
    listing = listing[jax.random.permutation(jax.random.fold_in(own, 1), rows)]
    offset_by = jax.random.randint(jax.random.fold_in(own, 2), (rows, 1), 0, top)
    return jnp.take_along_axis(listing, (jnp.arange(top)[None, :] + offset_by) % top, axis=1)


def load_shares(count, total, most, slope, full):
    weights = [(1 << 20) // math.isqrt(standing ** slope) + 1 for standing in range(1, count + 1)]
    largest = most if full else min(most, max(-(-total // count), total * weights[0] // sum(weights)))
    least = 1 if total - largest >= count - 1 else 0
    holding, spare = [largest] + [least] * (count - 1), total - largest - least * (count - 1)
    while spare > 0:
        movable = [i for i in range(1, count) if holding[i] < largest] or [i for i in range(1, count) if holding[i] < most]
        whole, remaining = sum([weights[i] for i in movable]), spare
        for i in movable:
            addition = min(most - holding[i], max(1, remaining * weights[i] // whole), spare)
            holding[i] = holding[i] + addition
            spare = spare - addition
    return np.array(holding)


def bell_draw(key, shape, width, most, shards=(), kind=jnp.bfloat16):
    factor_of = shard_levels(key, shape, shards, -0.22, 0.18) if shards else 1.0
    result = jax.random.normal(key, shape, jnp.float32) * width * factor_of
    return jnp.minimum(jnp.maximum(result, -most), most).astype(kind)


def setup_inputs(seed: int = 0) -> dict:
    splits = jax.random.split(jax.random.key(seed), 8)
    tokens = bell_draw(splits[0], (TOKENS, D), 1.0, 6.0, ((0, 128),))
    out_grad = bell_draw(splits[1], (TOKENS, D), 1.0, 6.0, ((0, 128),))
    expert_ids_keys = jax.random.split(jax.random.fold_in(splits[2], 1), TOKENS // TOK_DEV)
    expert_ids_turns = jax.random.permutation(jax.random.fold_in(splits[2], 3), TOKENS // TOK_DEV)
    expert_ids = jax.vmap(lambda own, number: shared_out(jax.random.fold_in(splits[2], 2), own, number, TOK_DEV, EXPERTS, TOPK, CAP, 2))(expert_ids_keys, expert_ids_turns).reshape((TOKENS, TOPK))
    gates = jnp.clip(jnp.exp(math.log(1.0) - 2.3025851 * jax.random.uniform(splits[3], (TOKENS, TOPK), jnp.float32) ** shard_levels(splits[3], (TOKENS, TOPK), ((0, 128),), -0.2, 0.2)), 0.1, 1.0)
    w_gate = bell_draw(splits[4], (EXPERTS, FF, D), D ** -0.5, 0.125, ((0, 32), (1, 4)))
    w_up = bell_draw(splits[5], (EXPERTS, FF, D), D ** -0.5, 0.125, ((0, 32), (1, 4)))
    w_down = bell_draw(splits[6], (EXPERTS, FF, D), FF ** -0.5, 0.15625, ((0, 32), (1, 4)))
    return {"tokens": tokens, "out_grad": out_grad, "expert_ids": expert_ids, "gates": gates, "w_gate": w_gate, "w_up": w_up, "w_down": w_down}


def expert_rows(x_rows, u_rows, w_gate_rows, w_up_rows, w_down_rows):
    last = (((1,), (1,)), ((), ()))
    first = (((0,), (0,)), ((), ()))
    pre_gate = lax.dot_general(x_rows, w_gate_rows, last, preferred_element_type=jnp.float32)
    pre_up = lax.dot_general(x_rows, w_up_rows, last, preferred_element_type=jnp.float32)
    sigma = jax.nn.sigmoid(pre_gate)
    active = pre_gate * sigma
    hidden = (active * pre_up).astype(jnp.bfloat16)
    grad_hidden = lax.dot_general(u_rows, w_down_rows, last, preferred_element_type=jnp.float32)
    grad_gate_pre = (grad_hidden * pre_up * sigma * (1.0 + pre_gate * (1.0 - sigma))).astype(jnp.bfloat16)
    grad_up_pre = (grad_hidden * active).astype(jnp.bfloat16)
    input_grad = jnp.dot(grad_gate_pre, w_gate_rows, preferred_element_type=jnp.float32) + jnp.dot(grad_up_pre, w_up_rows, preferred_element_type=jnp.float32)
    gate_term = lax.dot_general(grad_gate_pre, x_rows, first, preferred_element_type=jnp.float32)
    up_term = lax.dot_general(grad_up_pre, x_rows, first, preferred_element_type=jnp.float32)
    down_term = lax.dot_general(hidden, u_rows, first, preferred_element_type=jnp.float32)
    return input_grad, gate_term, up_term, down_term


def reference(tokens, out_grad, expert_ids, gates, w_gate, w_up, w_down):
    group_tokens = TOKENS // N_DP
    rows = N_EXPERT * CAP
    slot_ids = expert_ids.reshape(N_DP, group_tokens * TOPK)
    slot_gates = gates.reshape(N_DP, group_tokens * TOPK)

    def one_expert(carry, expert):
        gate_rows = w_gate[expert]
        up_rows = w_up[expert]
        down_rows = w_down[expert]
        totals = jnp.zeros((3, FF, D), jnp.float32)
        for group in range(N_DP):
            hits = slot_ids[group] == expert
            chosen = jnp.nonzero(hits, size=rows, fill_value=0)[0].astype(jnp.int32)
            count = jnp.sum(hits.astype(jnp.int32))
            valid = jnp.arange(rows, dtype=jnp.int32) < count
            token = (group * group_tokens + chosen // TOPK).astype(jnp.int32)
            x_rows = jnp.where(valid[:, None], tokens[token], jnp.zeros((), jnp.bfloat16))
            scaled = (out_grad[token].astype(jnp.float32) * slot_gates[group][chosen][:, None]).astype(jnp.bfloat16)
            u_rows = jnp.where(valid[:, None], scaled, jnp.zeros((), jnp.bfloat16))
            input_grad, gate_term, up_term, down_term = expert_rows(x_rows, u_rows, gate_rows, up_rows, down_rows)
            partial_sum = lax.optimization_barrier(jnp.stack([gate_term, up_term, down_term]).astype(jnp.bfloat16))
            totals = totals + partial_sum.astype(jnp.float32)
            slot_grad = lax.optimization_barrier(input_grad.astype(jnp.bfloat16)).astype(jnp.float32)
            slot_grad = jnp.where(valid[:, None], slot_grad, jnp.zeros((), jnp.float32))
            carry = carry.at[token].add(slot_grad)
        return carry, totals.astype(jnp.bfloat16)

    start = jnp.zeros((TOKENS, D), jnp.float32)
    summed, grads = lax.scan(one_expert, start, jnp.arange(EXPERTS, dtype=jnp.int32))
    return summed.astype(jnp.bfloat16), grads[:, 0], grads[:, 1], grads[:, 2]
```

```python
import jax
import jax.numpy as jnp
from jax import lax
from jax.sharding import PartitionSpec as P

f32, bf16 = jnp.float32, jnp.bfloat16
BOTH = ("dp", "expert")


def dot(a, b, ca, cb):
    return lax.dot_general(a, b, (((ca,), (cb,)), ((), ())), preferred_element_type=f32)


def partners(n_dp, n_expert):
    a, b = [], []
    for d in range(n_dp):
        for e in range(n_expert):
            near, wrap = d ^ 1, n_dp - 1 - d
            first, second = (near, wrap) if e % 2 == 0 else (wrap, near)
            a.append((d * n_expert + e, first * n_expert + e))
            b.append((d * n_expert + e, second * n_expert + e))
    return a, b


def forward(x, u, wg, wu, wd):
    pre_gate = dot(wg, x, 1, 1)
    pre_up = dot(wu, x, 1, 1)
    sigma = jax.nn.sigmoid(pre_gate)
    active = pre_gate * sigma
    hidden = (active * pre_up).astype(bf16)
    grad_hidden = dot(wd, u, 1, 1)
    dgate = (grad_hidden * pre_up * sigma * (1.0 + pre_gate * (1.0 - sigma))).astype(bf16)
    dup = (grad_hidden * active).astype(bf16)
    return dgate, dup, hidden


def shards(tokens, out_grad, expert_ids, gates, w_gate, w_up, w_down):
    owners = lax.axis_size("expert")
    a_pairs, b_pairs = partners(lax.axis_size("dp"), owners)
    swap_a = lambda v: lax.ppermute(v, BOTH, a_pairs)
    swap_b = lambda v: lax.ppermute(v, BOTH, b_pairs)

    mine = (w_gate[0], w_up[0], w_down[0])
    block = mine[0].shape[0]
    weights = [jnp.concatenate([w, swap_a(w)], axis=0) for w in mine]

    tok_count, width = tokens.shape
    topk = expert_ids.shape[1]
    cap = min(tok_count, 5 * topk * tok_count // (3 * owners))
    slots = tok_count * topk
    flat_ids = expert_ids.reshape(slots)
    onehot = (flat_ids[:, None] == jnp.arange(owners, dtype=jnp.int32)[None, :]).astype(jnp.int32)
    before = jnp.cumsum(onehot, axis=0) - onehot
    position = jnp.sum(before * onehot, axis=1)
    dest = flat_ids * cap + position
    source_of = jnp.full((owners * cap,), -1, jnp.int32).at[dest].set(jnp.arange(slots, dtype=jnp.int32))
    filled = (source_of >= 0)[:, None]
    source = jnp.maximum(source_of, 0)
    send_x = jnp.where(filled, tokens[source // topk], jnp.zeros((), bf16))
    scaled = (out_grad[source // topk].astype(f32) * gates.reshape(slots)[source][:, None]).astype(bf16)
    send_u = jnp.where(filled, scaled, jnp.zeros((), bf16))
    swap = lambda v: lax.all_to_all(v, "expert", split_axis=0, concat_axis=0, tiled=True)
    x0 = swap(send_x)
    u0 = swap(send_u)
    x1, u1 = swap_b(x0), swap_b(u0)

    g1, p1, h1 = forward(x1, u1, *weights)
    g0, p0, h0 = forward(x0, u0, *weights)
    away = dot(g1, weights[0], 0, 0) + dot(p1, weights[1], 0, 0)
    away = swap_b(away.astype(bf16))
    kept = dot(g0, weights[0], 0, 0) + dot(p0, weights[1], 0, 0)
    back = swap((kept + away.astype(f32)).astype(bf16))

    def weight_grads(part):
        pairs = ((g0, g1, x0, x1), (p0, p1, x0, x1), (h0, h1, u0, u1))
        return [dot(l0[part], r0, 1, 0) + dot(l1[part], r1, 1, 0) for l0, l1, r0, r1 in pairs]

    sent = [swap_a(v.astype(bf16)) for v in weight_grads(slice(block, None))]
    own = weight_grads(slice(0, block))
    grads = [(o + s.astype(f32)).astype(bf16)[None] for o, s in zip(own, sent)]
    slot_values = back[dest].astype(f32).reshape(tok_count, topk, width)
    grad_tokens = jnp.sum(slot_values, axis=1).astype(bf16)
    return (grad_tokens, *grads)


def solution(mesh):
    rows = P(BOTH, None)
    blocks = P("expert", "dp", None)
    return jax.shard_map(
        shards,
        mesh=mesh,
        in_specs=(rows, rows, rows, rows, blocks, blocks, blocks),
        out_specs=(rows, blocks, blocks, blocks),
        check_vma=False,
    )
```

```python
import jax
import jax.numpy as jnp
from jax import lax
from jax.experimental import pallas as pl
from jax.experimental.pallas import tpu as pltpu
from jax.sharding import PartitionSpec as P

f32, bf16 = jnp.float32, jnp.bfloat16
BOTH = ("dp", "expert")
RING = 4
BLOCK = 4
META = 8

EDGES = (
    ((0, 0), (1, 0)), ((0, 0), (3, 0)), ((0, 0), (0, 1)), ((0, 0), (0, 3)),
    ((0, 1), (1, 0)), ((0, 3), (3, 0)), ((3, 0), (0, 1)), ((1, 0), (0, 3)),
    ((1, 1), (1, 0)), ((3, 3), (3, 0)), ((1, 1), (0, 1)), ((3, 3), (0, 3)),
    ((1, 0), (1, 0)), ((0, 1), (0, 1)), ((3, 2), (3, 0)),
)
OFFSETS = tuple((i // RING, i % RING) for i in range(RING * RING))


def dot(a, b, ca, cb):
    return lax.dot_general(a, b, (((ca,), (cb,)), ((), ())), preferred_element_type=f32)


def after(offset, step):
    return ((offset[0] + step[0]) % RING, (offset[1] + step[1]) % RING)


def shift(value, step):
    pairs = []
    for e in range(2 * RING * RING):
        z, y = after((e // 8, e // 2 % 4), step)
        pairs.append((e, z * 8 + y * 2 + e % 2))
    return lax.ppermute(value, "expert", pairs)


def gather_plane(value):
    held = {(0, 0): value}
    for offset, step in EDGES:
        held[after(offset, step)] = shift(held[offset], step)
    return [held[o] for o in OFFSETS]


def reduce_plane(values):
    held = dict(zip(OFFSETS, values))
    for offset, step in reversed(EDGES):
        back = ((-step[0]) % RING, (-step[1]) % RING)
        moved = shift(held.pop(after(offset, step)), back)
        held[offset] = (held[offset].astype(f32) + moved.astype(f32)).astype(bf16)
    return held[0, 0]


def swap_core(value):
    return lax.ppermute(value, "expert", [(e, e ^ 1) for e in range(2 * RING * RING)])


def partners(n_dp, n_expert):
    a, b = [], []
    for d in range(n_dp):
        for e in range(n_expert):
            near, wrap = d ^ 1, n_dp - 1 - d
            first, second = (near, wrap) if e % 2 == 0 else (wrap, near)
            a.append((d * n_expert + e, first * n_expert + e))
            b.append((d * n_expert + e, second * n_expert + e))
    return a, b


def select_x_kernel(cap, who, *refs):
    count = RING * RING
    shards, (own, other, sel, gcol) = refs[:count], refs[count:]
    toks = shards[0].shape[0] - META
    rows, wide = BLOCK * cap, BLOCK * toks
    groups = count // BLOCK

    @pl.when(pl.program_id(0) == 0)
    def _():
        lane = lax.broadcasted_iota(jnp.int32, (META, 2 * toks), 1)
        lower = lax.broadcasted_iota(jnp.int32, (wide, wide), 0)
        upper = lax.broadcasted_iota(jnp.int32, (wide, wide), 1)
        earlier = jnp.where(lower < upper, 1.0, 0.0).astype(bf16)
        index = lax.broadcasted_iota(jnp.int32, (rows, wide), 0).astype(f32)

        def meta(group, column):
            parts = []
            for first in range(group * BLOCK, (group + 1) * BLOCK, 2):
                left, right = [
                    shards[first + i][toks : toks + META, column : column + 2 * toks].astype(f32)
                    for i in range(2)
                ]
                parts.append(jnp.where(lane < toks, left, right))
            return jnp.concatenate(parts, axis=1)

        for group in range(groups):
            ids = meta(group, 0)
            gate = meta(group, 2 * toks) + meta(group, 4 * toks)
            for side in range(2):
                match = ids == who[side].astype(f32)
                hit = jnp.sum(jnp.where(match, 1.0, 0.0), axis=0, keepdims=True)
                weight = jnp.sum(jnp.where(match, gate, 0.0), axis=0, keepdims=True)
                rank = dot(jnp.broadcast_to(hit, (16, wide)).astype(bf16), earlier, 1, 0)[0:1]
                chosen = jnp.where((rank == index) & (hit > 0.0), 1.0, 0.0)
                part = pl.ds(side * rows, rows)
                sel[group, part, :] = chosen.astype(bf16)
                total = jnp.sum(chosen * weight, axis=1, keepdims=True)
                gcol[group, part, :] = jnp.broadcast_to(total, (rows, 128))

    for group in range(groups):
        block = jnp.concatenate([shards[group * BLOCK + i][0:toks, :] for i in range(BLOCK)], axis=0)
        picked = dot(sel[group], block, 1, 0).astype(bf16)
        own[pl.ds(group * rows, rows), :] = picked[:rows]
        other[pl.ds(group * rows, rows), :] = picked[rows:]


def select_u_kernel(cap, sel, gcol, *refs):
    count = RING * RING
    shards, (own, other) = refs[:count], refs[count:]
    rows = BLOCK * cap
    for group in range(count // BLOCK):
        block = jnp.concatenate([shards[group * BLOCK + i][...] for i in range(BLOCK)], axis=0)
        picked = dot(sel[group], block, 1, 0) * gcol[group, :, 0:1]
        picked = picked.astype(bf16)
        own[pl.ds(group * rows, rows), :] = picked[:rows]
        other[pl.ds(group * rows, rows), :] = picked[rows:]


def scatter_kernel(cap, sel, own, other, *outs):
    rows = BLOCK * cap
    toks = outs[0].shape[0]
    for group in range(len(outs) // BLOCK):
        part = pl.ds(group * rows, rows)
        both = jnp.concatenate([own[part, :], other[part, :]], axis=0)
        dense = dot(sel[group], both, 0, 0).astype(bf16)
        for i in range(BLOCK):
            outs[group * BLOCK + i][...] = dense[i * toks : (i + 1) * toks]


def column(height, wide):
    return pl.BlockSpec((height, wide), lambda j, *_: (0, j))


def whole(*dims):
    return pl.BlockSpec(dims, lambda j, *_: (0,) * len(dims))


def cost(flops, moved):
    return pl.CostEstimate(flops=flops, bytes_accessed=moved, transcendentals=0)


def select_x(who, shards, cap):
    height, width = shards[0].shape
    toks = height - META
    wide, groups, rows = min(512, width), len(shards) // BLOCK, BLOCK * cap
    picked = jax.ShapeDtypeStruct((groups * rows, width), bf16)
    return pl.pallas_call(
        lambda *refs: select_x_kernel(cap, *refs),
        grid_spec=pltpu.PrefetchScalarGridSpec(
            num_scalar_prefetch=1,
            grid=(width // wide,),
            in_specs=[column(height, wide)] * len(shards),
            out_specs=[column(groups * rows, wide)] * 2
            + [whole(groups, 2 * rows, BLOCK * toks), whole(groups, 2 * rows, 128)],
        ),
        out_shape=[picked, picked]
        + [
            jax.ShapeDtypeStruct((groups, 2 * rows, BLOCK * toks), bf16),
            jax.ShapeDtypeStruct((groups, 2 * rows, 128), f32),
        ],
        cost_estimate=cost(4 * groups * rows * BLOCK * toks * width, 8 * groups * rows * width),
        name="select_x",
    )(who, *shards)


def select_u(sel, gcol, shards, cap):
    toks, width = shards[0].shape
    wide, groups, rows = min(512, width), len(shards) // BLOCK, BLOCK * cap
    picked = jax.ShapeDtypeStruct((groups * rows, width), bf16)
    return pl.pallas_call(
        lambda *refs: select_u_kernel(cap, *refs),
        grid=(width // wide,),
        in_specs=[whole(*sel.shape), whole(*gcol.shape)] + [column(toks, wide)] * len(shards),
        out_specs=[column(groups * rows, wide)] * 2,
        out_shape=[picked, picked],
        cost_estimate=cost(4 * groups * rows * BLOCK * toks * width, 8 * groups * rows * width),
        name="select_u",
    )(sel, gcol, *shards)


def scatter(sel, own, other, toks, cap):
    height, width = own.shape
    wide, count = min(512, width), RING * RING
    return pl.pallas_call(
        lambda *refs: scatter_kernel(cap, *refs),
        grid=(width // wide,),
        in_specs=[whole(*sel.shape), column(height, wide), column(height, wide)],
        out_specs=[column(toks, wide)] * count,
        out_shape=[jax.ShapeDtypeStruct((toks, width), bf16)] * count,
        cost_estimate=cost(4 * height * BLOCK * toks * width, 8 * height * width),
        name="scatter",
    )(sel, own, other)


def forward(x, u, wg, wu, wd):
    pre_gate = dot(wg, x, 1, 1)
    pre_up = dot(wu, x, 1, 1)
    sigma = jax.nn.sigmoid(pre_gate)
    active = pre_gate * sigma
    hidden = (active * pre_up).astype(bf16)
    grad_hidden = dot(wd, u, 1, 1)
    dgate = (grad_hidden * pre_up * sigma * (1.0 + pre_gate * (1.0 - sigma))).astype(bf16)
    dup = (grad_hidden * active).astype(bf16)
    return dgate, dup, hidden


def with_meta(tokens, expert_ids, gates):
    ids = expert_ids.T.astype(f32)
    high = lax.reduce_precision(gates.T, 8, 7)
    low = gates.T - high
    parts = jnp.concatenate([ids, ids, high, high, low, low], axis=1)
    parts = jnp.pad(
        parts,
        ((0, META - parts.shape[0]), (0, tokens.shape[1] - parts.shape[1])),
        constant_values=-1.0,
    )
    return jnp.concatenate([tokens, parts.astype(bf16)], axis=0)


def shards(tokens, out_grad, expert_ids, gates, w_gate, w_up, w_down):
    owners = lax.axis_size("expert")
    a_pairs, b_pairs = partners(lax.axis_size("dp"), owners)
    swap_a = lambda v: lax.ppermute(v, BOTH, a_pairs)
    swap_b = lambda v: lax.ppermute(v, BOTH, b_pairs)
    toks, width = tokens.shape
    topk = expert_ids.shape[1]
    cap = min(toks, 5 * topk * toks // (3 * owners))
    me = lax.axis_index("expert").astype(jnp.int32)
    who = jnp.stack([me, me ^ 1])

    held_x = gather_plane(with_meta(tokens, expert_ids, gates))
    mine = (w_gate[0], w_up[0], w_down[0])
    block = mine[0].shape[0]
    weights = [jnp.concatenate([w, swap_a(w)], axis=0) for w in mine]
    held_u = gather_plane(out_grad)

    x_own, x_other, sel, gcol = select_x(who, held_x, cap)
    x0 = jnp.concatenate([x_own, swap_core(x_other)], axis=0)
    x1 = swap_b(x0)
    u_own, u_other = select_u(sel, gcol, held_u, cap)
    u0 = jnp.concatenate([u_own, swap_core(u_other)], axis=0)
    u1 = swap_b(u0)

    g0, p0, h0 = forward(x0, u0, *weights)
    g1, p1, h1 = forward(x1, u1, *weights)
    away = dot(g1, weights[0], 0, 0) + dot(p1, weights[1], 0, 0)
    away = swap_b(away.astype(bf16))
    kept = dot(g0, weights[0], 0, 0) + dot(p0, weights[1], 0, 0)

    def weight_grads(part):
        pairs = ((g0, g1, x0, x1), (p0, p1, x0, x1), (h0, h1, u0, u1))
        return [dot(l0[part], r0, 1, 0) + dot(l1[part], r1, 1, 0) for l0, l1, r0, r1 in pairs]

    sent = [swap_a(v.astype(bf16)) for v in weight_grads(slice(block, None))]
    own = weight_grads(slice(0, block))
    grads = [(o + s.astype(f32)).astype(bf16)[None] for o, s in zip(own, sent)]

    slot_grads = (kept + away.astype(f32)).astype(bf16)
    half = slot_grads.shape[0] // 2
    other = swap_core(slot_grads[half:])
    grad_tokens = reduce_plane(scatter(sel, slot_grads[:half], other, toks, cap))
    return (grad_tokens, *grads)


def solution(mesh):
    rows = P(BOTH, None)
    blocks = P("expert", "dp", None)
    return jax.shard_map(
        shards,
        mesh=mesh,
        in_specs=(rows, rows, rows, rows, blocks, blocks, blocks),
        out_specs=(rows, blocks, blocks, blocks),
        check_vma=False,
    )
```
